32 devices in a mesh: grp: 2 (over x), chan: 16 (over z, y, core).
Axes of the slice: x: 2, y: 2, z: 4, core: 2. Of those that a mesh axis runs over, the one named last changes fastest.
Arguments:
- spectra: bfloat16 [2048, 2, 64, 512], P(('grp', 'chan')), parts along dimension 0, may hold values from -6 to 6
- valid: int32 [2048, 64], P(('grp', 'chan')), parts along dimension 0, may hold values 0 or 1
- sources: int32 [32], P('grp'), parts along dimension 0, may hold values from 0 to 1023
Outputs:
- smoothed: float32 [32, 1024, 1024], P('grp', 'chan'), parts along dimension 0
The draws below stay inside these ranges and needn't reach their ends.
There are 2 independent parts, one for each index of `grp`. The reference program is written for one: setup_inputs(seed, part) draws one part's arguments, and reference() takes and returns one part's arrays. A program takes and returns all parts, laid end to end along the dimension named above; each array names one. Nothing has to cross between parts.
Inputs may be any that keep to these rules, and one draw needn't show every extreme that they name: `sources`: channel indices of the segment; repeats may occur.
All inputs are finite; a program needn't handle non-finite values. No bound on the sum of `valid` on one device may be relied on, other than what follows from the above.
Results may differ from the reference program's by a relative error of at most 0.0037.
Values may be sent and summed in bfloat16 or wider, within the bound.
A program may use at most 128 MiB of HBM per device.

```python
import jax
import jax.numpy as jnp
from jax import lax

F = 512
S = 16
W = 64
CH_DEV = 64
CHANNELS = 1024
NL = 1024


def place_ends(drawn, rng, low, high):
    shape = drawn.shape
    place = [jax.random.randint(jax.random.fold_in(rng, axis), (), 0, shape[axis]) for axis in range(len(shape))]
    drawn = drawn.at[tuple(place)].set(low)
    longest = shape.index(max(shape))
    place[longest] = (place[longest] + 1) % shape[longest]
    return drawn.at[tuple(place)].set(high)


def levels(rng, extent, cuts, smallest, largest):
    factor_of = 1.0
    for axis_at, shards_of in cuts:
        draws = jax.random.uniform(jax.random.fold_in(jax.random.fold_in(rng, 6), axis_at), (shards_of,), jnp.float32, smallest / len(cuts), largest / len(cuts))
        factor_of = factor_of * jnp.repeat(jnp.exp(draws), extent[axis_at] // shards_of).reshape((-1,) + (1,) * (len(extent) - 1 - axis_at))
    return factor_of


def centred(stream_key, extent, width, limit, shards=(), kind=jnp.bfloat16):
    array = jax.random.normal(stream_key, extent, jnp.float32) * width
    if len(shards) > 0:
        array = levels(stream_key, extent, shards, -0.22, 0.18) * array
    return jnp.clip(array, min=-limit, max=limit).astype(kind)


def setup_inputs(seed: int = 0, part: int = 0) -> dict:
    splits = jax.random.split(jax.random.key(seed), 4)
    part_splits = jax.random.split(jax.random.fold_in(splits[3], part), 4)
    return {
        "spectra": centred(part_splits[0], (CHANNELS, 2, W, F), 1.0, 6.0, ((0, 16),)),
        "valid": place_ends((jax.random.randint(part_splits[1], (CHANNELS, W), 0, 4) < 3).astype(jnp.int32), jax.random.fold_in(part_splits[1], 1), 0, 1),
        "sources": place_ends(jax.random.randint(part_splits[2], (S,), 0, CHANNELS), jax.random.fold_in(part_splits[2], 1), 0, CHANNELS - 1).astype(jnp.int32),
    }


def make_table(nbins, nlags):
    freq = jnp.arange(nbins, dtype=jnp.int32)
    lagidx = jnp.arange(nlags, dtype=jnp.int32)
    phase = ((freq[:, None] * lagidx[None, :]) % nlags).astype(jnp.float32)
    angle = 2.0 * jnp.pi * phase / nlags
    weight = jnp.where(freq == 0, 1.0, 2.0).astype(jnp.float32) / nlags
    cosine = weight[:, None] * jnp.cos(angle)
    sine = -weight[:, None] * jnp.sin(angle)
    return jnp.concatenate([cosine, sine], axis=0).astype(jnp.bfloat16)


def reference(spectra, valid, sources):
    src_spec = spectra[sources].astype(jnp.float32)
    src_valid = valid[sources].astype(jnp.float32)
    src_m = src_spec * src_valid[:, None, :, None]
    table = make_table(F, NL)
    blocks = CHANNELS // CH_DEV
    spec_blocks = spectra.reshape(blocks, CH_DEV, 2, W, F)
    valid_blocks = valid.reshape(blocks, CH_DEV, W)

    def one_block(pair):
        spec_b, valid_b = pair
        chan_m = spec_b.astype(jnp.float32) * valid_b.astype(jnp.float32)[:, None, :, None]
        aa = jnp.einsum('swf,cwf->scf', src_m[:, 0], chan_m[:, 0])
        bb = jnp.einsum('swf,cwf->scf', src_m[:, 1], chan_m[:, 1])
        ad = jnp.einsum('swf,cwf->scf', src_m[:, 0], chan_m[:, 1])
        bc = jnp.einsum('swf,cwf->scf', src_m[:, 1], chan_m[:, 0])
        cross = jnp.concatenate([(aa + bb) / W, (ad - bc) / W], axis=2).astype(jnp.bfloat16)
        flat = cross.reshape(S * CH_DEV, 2 * F)
        return jnp.dot(flat, table, preferred_element_type=jnp.float32).reshape(S, CH_DEV, NL)

    lag_blocks = lax.map(one_block, (spec_blocks, valid_blocks))
    lags = jnp.transpose(lag_blocks, (1, 0, 2, 3)).reshape(S, CHANNELS, NL)
    padded = jnp.pad(lags, ((0, 0), (2, 2), (0, 0)))
    total = padded[:, 0:CHANNELS] + padded[:, 1:CHANNELS + 1] + padded[:, 2:CHANNELS + 2]
    total = total + padded[:, 3:CHANNELS + 3] + padded[:, 4:CHANNELS + 4]
    return total / 5.0
```

```python
import functools

import jax
import jax.numpy as jnp
import numpy as np
from jax import lax
from jax.experimental import pallas as pl
from jax.experimental.pallas import tpu as pltpu
from jax.sharding import PartitionSpec as P

MESH = pl.DeviceIdType.MESH
HALO = 2


def make_table(nbins, nlags):
    freq = np.arange(nbins, dtype=np.int64)
    phase = (freq[:, None] * np.arange(nlags, dtype=np.int64)[None, :]) % nlags
    angle = 2.0 * np.pi * phase / nlags
    weight = np.where(freq == 0, 1.0, 2.0) / nlags
    table = np.concatenate([weight[:, None] * np.cos(angle), -weight[:, None] * np.sin(angle)])
    return table.astype(np.float32).astype(jnp.bfloat16)


def pick_kernel(nsrc, src_ref, mask_ref, spec_ref, out_ref, buf, sems):
    nchan = spec_ref.shape[0]
    me = lax.axis_index("chan")
    spots, copies = [], []
    for row in range(nsrc + 2 * HALO):
        if row < nsrc:
            spot = src_ref[row] - me * nchan
        else:
            spot = row - nsrc if row < nsrc + HALO else nchan - 2 * HALO + row - nsrc
        held = jnp.clip(spot, 0, nchan - 1) if row < nsrc else spot
        copy = pltpu.make_async_copy(spec_ref.at[held], buf.at[row], sems.at[row])
        copy.start()
        spots.append(spot)
        copies.append(copy)
    mask = mask_ref[...]
    lane = lax.broadcasted_iota(jnp.int32, mask.shape, 1)
    for row, (spot, copy) in enumerate(zip(spots, copies)):
        column = jnp.sum(jnp.where(lane == spot, mask, 0.0), axis=1, keepdims=True)
        copy.wait()
        out_ref[row] = (buf[row].astype(jnp.float32) * column).astype(out_ref.dtype)


def share_kernel(outer, inner, nchunk, pick_ref, edge_ref, out_ref, halo_ref, part, first, second,
                 ins, outs, send_sem, recv_sem, edge_send, edge_recv):
    half = nchunk // 2
    size = outer * inner * 2
    me = lax.axis_index("chan")
    core, chip = me % 2, me // 2
    j, i = chip % inner, chip // inner
    lines = ((j, inner, 2), (i, outer, 2 * inner))
    partner = me + 1 - 2 * core

    barrier = pltpu.get_barrier_semaphore()

    def greet(there):
        pl.semaphore_signal(barrier, inc=1, device_id={"chan": there}, device_id_type=MESH)

    greet(partner)
    count = jnp.int32(1)
    for pos, length, stride in lines + ((me, size, 1),):
        @pl.when(pos > 0)
        def _():
            greet(me - stride)

        @pl.when(pos < length - 1)
        def _():
            greet(me + stride)

        count = count + (pos > 0).astype(jnp.int32) + (pos < length - 1).astype(jnp.int32)
    pl.semaphore_wait(barrier, count)

    def remote(src, dst, kind, k, there):
        return pltpu.make_async_remote_copy(
            src_ref=src, dst_ref=dst, send_sem=send_sem.at[kind, k], recv_sem=recv_sem.at[kind, k],
            device_id={"chan": there}, device_id_type=MESH)

    def across(k):
        return remote(pick_ref.at[(1 - core) * half + k], part.at[k], 0, k, partner)

    def back(k):
        spot = core * half + k
        return remote(out_ref.at[spot], out_ref.at[spot], 1, k, partner)

    def hop(line, up, src, k):
        pos, length, stride = lines[line]
        kind = 2 + 2 * line + (0 if up else 1)
        there = me + stride if up else me - stride
        return remote(src, ins.at[kind - 2, k], kind, k, there)

    def to_after():
        return pltpu.make_async_remote_copy(
            src_ref=edge_ref.at[pl.ds(HALO, HALO)], dst_ref=halo_ref.at[pl.ds(0, HALO)],
            send_sem=edge_send.at[0], recv_sem=edge_recv.at[0],
            device_id={"chan": me + 1}, device_id_type=MESH)

    def to_before():
        return pltpu.make_async_remote_copy(
            src_ref=edge_ref.at[pl.ds(0, HALO)], dst_ref=halo_ref.at[pl.ds(HALO, HALO)],
            send_sem=edge_send.at[1], recv_sem=edge_recv.at[1],
            device_id={"chan": me - 1}, device_id_type=MESH)

    def begin(line, x, k):
        pos, length, _ = lines[line]
        if length == 1:
            return

        @pl.when(pos == 0)
        def _():
            hop(line, True, x.at[k], k).start()

        @pl.when(pos == length - 1)
        def _():
            hop(line, False, x.at[k], k).start()

    def finish(line, x, k, total, at):
        pos, length, _ = lines[line]
        if length == 1:
            total[at] = x[k]
            return
        low, high = ins.at[2 * line], ins.at[2 * line + 1]

        @pl.when(pos > 0)
        def _():
            hop(line, True, x.at[k], k).wait_recv()
            if length > 2:
                @pl.when(pos < length - 1)
                def _():
                    outs[2 * line, k] = x[k] + low[k]
                    hop(line, True, outs.at[2 * line, k], k).start()

        @pl.when(pos < length - 1)
        def _():
            hop(line, False, x.at[k], k).wait_recv()
            if length > 2:
                @pl.when(pos > 0)
                def _():
                    outs[2 * line + 1, k] = x[k] + high[k]
                    hop(line, False, outs.at[2 * line + 1, k], k).start()

        @pl.when(pos == 0)
        def _():
            total[at] = x[k] + high[k]

        @pl.when(pos == length - 1)
        def _():
            total[at] = x[k] + low[k]

        if length > 2:
            @pl.when((pos > 0) & (pos < length - 1))
            def _():
                total[at] = x[k] + low[k] + high[k]

    def send_across(k, carry):
        across(k).start()
        return carry

    lax.fori_loop(0, half, send_across, 0)

    @pl.when(me < size - 1)
    def _():
        to_after().start()

    @pl.when(me > 0)
    def _():
        to_before().start()

    @pl.when(me == 0)
    def _():
        halo_ref[0:HALO] = jnp.zeros((HALO,) + halo_ref.shape[1:], halo_ref.dtype)

    @pl.when(me == size - 1)
    def _():
        halo_ref[HALO:] = jnp.zeros((HALO,) + halo_ref.shape[1:], halo_ref.dtype)

    def step(t, carry):
        @pl.when(t < half)
        def _():
            across(t).wait_recv()
            first[t] = pick_ref[core * half + t] + part[t]
            begin(0, first, t)

        @pl.when((t >= 1) & (t < half + 1))
        def _():
            finish(0, first, t - 1, second, t - 1)
            begin(1, second, t - 1)

        @pl.when(t >= 2)
        def _():
            finish(1, second, t - 2, out_ref, core * half + t - 2)
            back(t - 2).start()

        return carry

    lax.fori_loop(0, half + 2, step, 0)

    def close(k, carry):
        across(k).wait_send()
        other = (1 - core) * half + k
        remote(out_ref.at[other], out_ref.at[other], 1, k, partner).wait_recv()
        back(k).wait_send()
        for line, (pos, length, _) in enumerate(lines):
            if length == 1:
                continue

            @pl.when(pos < length - 1)
            def _():
                hop(line, True, first.at[k], k).wait_send()

            @pl.when(pos > 0)
            def _():
                hop(line, False, first.at[k], k).wait_send()

        return carry

    lax.fori_loop(0, half, close, 0)

    @pl.when(me < size - 1)
    def _():
        to_after().wait_send()
        to_before().wait_recv()

    @pl.when(me > 0)
    def _():
        to_before().wait_send()
        to_after().wait_recv()


def lag_kernel(nwin, nrow, sgroup, spec_ref, valid_ref, src_ref, halo_ref, table_ref, out_ref,
               chan_t, src_t, cross_t, lag):
    nchan, depth, fb = spec_ref.shape
    nsrc = src_ref.shape[0]
    nbins = table_ref.shape[0] // 2
    steps = nbins // fb
    at = pl.program_id(0)

    @pl.when(at < steps)
    def _():
        def turn(x):
            return jnp.transpose(x).astype(jnp.float32)

        for c in range(HALO):
            chan_t[c * fb:(c + 1) * fb] = turn(halo_ref[c])
            far = nchan + HALO + c
            chan_t[far * fb:(far + 1) * fb] = turn(halo_ref[HALO + c])

        def channel(c, carry):
            chan_t[pl.ds(pl.multiple_of((c + HALO) * fb, fb), fb)] = (
                turn(spec_ref[c]) * valid_ref[pl.ds(c, 1)])
            return carry

        lax.fori_loop(0, nchan, channel, 0, unroll=4)
        sign = jnp.where(lax.broadcasted_iota(jnp.int32, (1, depth), 1) < nwin, -1.0, 1.0)

        def source(s, carry):
            x = turn(src_ref[s])
            src_t[pl.ds(pl.multiple_of(s * fb, fb), fb)] = x
            src_t[pl.ds(pl.multiple_of((s + nsrc) * fb, fb), fb)] = (
                pltpu.roll(x, nwin, axis=1) * sign)
            return carry

        lax.fori_loop(0, nsrc, source, 0, unroll=2)

        def one(f, carry):
            right = chan_t[pl.ds(f, nrow, stride=fb)].astype(jnp.bfloat16)
            left = src_t[pl.ds(f, 2 * nsrc, stride=fb)].astype(jnp.bfloat16)
            both = lax.dot_general(left, right, (((1,), (1,)), ((), ())),
                                   preferred_element_type=jnp.float32)
            row = pl.multiple_of((at * fb + f) * 2 * nsrc, 2 * nsrc)
            cross_t[pl.ds(row, 2 * nsrc), 0:nrow] = both * (1.0 / nwin)
            return carry

        lax.fori_loop(0, fb, one, 0, unroll=8)

    @pl.when(at >= steps)
    def _():
        group = at - steps
        rows = []
        for q in range(sgroup):
            s = group * sgroup + q
            re = cross_t[pl.ds(s, nbins, stride=2 * nsrc)]
            im = cross_t[pl.ds(s + nsrc, nbins, stride=2 * nsrc)]
            flat = jnp.concatenate([re, im], axis=0).astype(jnp.bfloat16)
            rows.append(jnp.transpose(flat)[0:nrow])
        lag[...] = jnp.dot(jnp.concatenate(rows, axis=0), table_ref[...],
                           preferred_element_type=jnp.float32)
        for q in range(sgroup):
            base = q * nrow
            total = lag[base:base + nchan] + lag[base + 1:base + 1 + nchan]
            for k in range(2, 2 * HALO + 1):
                total = total + lag[base + k:base + k + nchan]
            out_ref[q] = total / (2 * HALO + 1.0)


def local(size, spectra, valid, sources):
    nchan, _, nwin, nbins = spectra.shape
    nsrc = sources.shape[0]
    depth, nlags = 2 * nwin, 2 * nbins
    spec = spectra.reshape(nchan, depth, nbins)
    flags = valid.astype(jnp.float32)
    flags2 = jnp.concatenate([flags, flags], axis=1)
    vmem = pl.BlockSpec(memory_space=pltpu.VMEM)

    picked = pl.pallas_call(
        functools.partial(pick_kernel, nsrc),
        out_shape=jax.ShapeDtypeStruct((nsrc + 2 * HALO, depth, nbins), jnp.bfloat16),
        in_specs=[pl.BlockSpec(memory_space=pltpu.SMEM), vmem, pl.BlockSpec(memory_space=pl.ANY)],
        out_specs=vmem,
        scratch_shapes=[pltpu.VMEM((nsrc + 2 * HALO, depth, nbins), jnp.bfloat16),
                        pltpu.SemaphoreType.DMA((nsrc + 2 * HALO,))],
        compiler_params=pltpu.CompilerParams(vmem_limit_bytes=24 << 20),
        name="pick",
    )(sources, flags2.T, spec)

    chips = size // 2
    inner = 1
    while (2 * inner) ** 2 <= chips and chips % (2 * inner) == 0:
        inner *= 2
    outer = chips // inner
    cut = 2
    nchunk, crow = nsrc * cut, depth // cut
    half = nchunk // 2
    chunk = lambda *lead: pltpu.VMEM(lead + (crow, nbins), jnp.bfloat16)
    src, halo = pl.pallas_call(
        functools.partial(share_kernel, outer, inner, nchunk),
        out_shape=[jax.ShapeDtypeStruct((nchunk, crow, nbins), jnp.bfloat16),
                   jax.ShapeDtypeStruct((2 * HALO, depth, nbins), jnp.bfloat16)],
        in_specs=[vmem, vmem],
        out_specs=[vmem, vmem],
        scratch_shapes=[chunk(half), chunk(half), chunk(half), chunk(4, half), chunk(4, half),
                        pltpu.SemaphoreType.DMA((6, half)), pltpu.SemaphoreType.DMA((6, half)),
                        pltpu.SemaphoreType.DMA((2,)), pltpu.SemaphoreType.DMA((2,))],
        compiler_params=pltpu.CompilerParams(
            collective_id=0, has_side_effects=True, vmem_limit_bytes=40 << 20),
        name="share",
    )(picked[:nsrc].reshape(nchunk, crow, nbins), picked[nsrc:])
    src = src.reshape(nsrc, depth, nbins)

    fb = 128
    steps = nbins // fb
    sgroup = 4 if nsrc % 4 == 0 else 1
    nrow = -(-(nchan + 2 * HALO) // 16) * 16
    by_f = lambda at: (0, 0, jnp.minimum(at, steps - 1))
    return pl.pallas_call(
        functools.partial(lag_kernel, nwin, nrow, sgroup),
        grid=(steps + nsrc // sgroup,),
        out_shape=jax.ShapeDtypeStruct((nsrc, nchan, nlags), jnp.float32),
        in_specs=[pl.BlockSpec((nchan, depth, fb), by_f),
                  pl.BlockSpec((nchan, depth), lambda at: (0, 0)),
                  pl.BlockSpec((nsrc, depth, fb), by_f),
                  pl.BlockSpec((2 * HALO, depth, fb), by_f),
                  pl.BlockSpec((nlags, nlags), lambda at: (0, 0))],
        out_specs=pl.BlockSpec((sgroup, nchan, nlags), lambda at: (jnp.maximum(at - steps, 0), 0, 0)),
        scratch_shapes=[pltpu.VMEM((nrow * fb, depth), jnp.float32),
                        pltpu.VMEM((2 * nsrc * fb, depth), jnp.float32),
                        pltpu.VMEM((nbins * 2 * nsrc, 128), jnp.float32),
                        pltpu.VMEM((sgroup * nrow, nlags), jnp.float32)],
        compiler_params=pltpu.CompilerParams(vmem_limit_bytes=56 << 20),
        name="lags",
    )(spec, flags2, src, halo, jnp.asarray(make_table(nbins, nlags)))


def solution(mesh):
    in_specs = (P(("grp", "chan"), None, None, None), P(("grp", "chan"), None), P("grp"))
    out_specs = P("grp", "chan", None)
    return jax.shard_map(functools.partial(local, mesh.shape["chan"]), mesh=mesh,
                         in_specs=in_specs, out_specs=out_specs, check_vma=False)
```

```python
import functools

import jax
import jax.numpy as jnp
import numpy as np
from jax import lax
from jax.experimental import pallas as pl
from jax.experimental.pallas import tpu as pltpu
from jax.sharding import PartitionSpec as P

MESH = pl.DeviceIdType.MESH
HALO = 2
LAG = 2


def make_table(nbins, nlags):
    freq = np.arange(nbins, dtype=np.int64)
    phase = (freq[:, None] * np.arange(nlags, dtype=np.int64)[None, :]) % nlags
    angle = 2.0 * np.pi * phase / nlags
    weight = np.where(freq == 0, 1.0, 2.0) / nlags
    table = np.concatenate([weight[:, None] * np.cos(angle), -weight[:, None] * np.sin(angle)])
    return table.astype(np.float32).astype(jnp.bfloat16)


def pick_kernel(nsrc, src_ref, mask_ref, spec_ref, out_ref, buf, sems):
    nchan = spec_ref.shape[0]
    me = lax.axis_index("chan")
    spots, copies = [], []
    for row in range(nsrc + 2 * HALO):
        if row < nsrc:
            spot = src_ref[row] - me * nchan
        else:
            spot = row - nsrc if row < nsrc + HALO else nchan - 2 * HALO + row - nsrc
        held = jnp.clip(spot, 0, nchan - 1) if row < nsrc else spot
        copy = pltpu.make_async_copy(spec_ref.at[held], buf.at[row], sems.at[row])
        copy.start()
        spots.append(spot)
        copies.append(copy)
    mask = mask_ref[...]
    lane = lax.broadcasted_iota(jnp.int32, mask.shape, 1)
    for row, (spot, copy) in enumerate(zip(spots, copies)):
        column = jnp.sum(jnp.where(lane == spot, mask, 0.0), axis=1, keepdims=True)
        copy.wait()
        out_ref[row] = (buf[row].astype(jnp.float32) * column).astype(out_ref.dtype)


def share_kernel(outer, inner, nchunk, pick_ref, edge_ref, out_ref, halo_ref, part, first, second,
                 ins, outs, send_sem, recv_sem, edge_send, edge_recv):
    half = nchunk // 2
    size = outer * inner * 2
    me = lax.axis_index("chan")
    core, chip = me % 2, me // 2
    j, i = chip % inner, chip // inner
    lines = ((j, inner, 2), (i, outer, 2 * inner))
    partner = me + 1 - 2 * core

    barrier = pltpu.get_barrier_semaphore()

    def greet(there):
        pl.semaphore_signal(barrier, inc=1, device_id={"chan": there}, device_id_type=MESH)

    greet(partner)
    count = jnp.int32(1)
    for pos, length, stride in lines + ((me, size, 1),):
        @pl.when(pos > 0)
        def _():
            greet(me - stride)

        @pl.when(pos < length - 1)
        def _():
            greet(me + stride)

        count = count + (pos > 0).astype(jnp.int32) + (pos < length - 1).astype(jnp.int32)
    pl.semaphore_wait(barrier, count)

    def remote(src, dst, kind, k, there):
        return pltpu.make_async_remote_copy(
            src_ref=src, dst_ref=dst, send_sem=send_sem.at[kind, k], recv_sem=recv_sem.at[kind, k],
            device_id={"chan": there}, device_id_type=MESH)

    def across(k):
        return remote(pick_ref.at[(1 - core) * half + k], part.at[k], 0, k, partner)

    def back(k):
        spot = core * half + k
        return remote(out_ref.at[spot], out_ref.at[spot], 1, k, partner)

    def hop(line, up, src, k):
        pos, length, stride = lines[line]
        kind = 2 + 2 * line + (0 if up else 1)
        there = me + stride if up else me - stride
        return remote(src, ins.at[kind - 2, k], kind, k, there)

    def to_after():
        return pltpu.make_async_remote_copy(
            src_ref=edge_ref.at[pl.ds(HALO, HALO)], dst_ref=halo_ref.at[pl.ds(0, HALO)],
            send_sem=edge_send.at[0], recv_sem=edge_recv.at[0],
            device_id={"chan": me + 1}, device_id_type=MESH)

    def to_before():
        return pltpu.make_async_remote_copy(
            src_ref=edge_ref.at[pl.ds(0, HALO)], dst_ref=halo_ref.at[pl.ds(HALO, HALO)],
            send_sem=edge_send.at[1], recv_sem=edge_recv.at[1],
            device_id={"chan": me - 1}, device_id_type=MESH)

    def begin(line, x, k):
        pos, length, _ = lines[line]
        if length == 1:
            return

        @pl.when(pos == 0)
        def _():
            hop(line, True, x.at[k], k).start()

        @pl.when(pos == length - 1)
        def _():
            hop(line, False, x.at[k], k).start()

    def guarded(k, also, run):
        @pl.when((k >= 0) & (k < half) & also)
        def _():
            run(k)

    def relay(line, x, t):
        pos, length, _ = lines[line]
        if length == 1:
            return

        def go(up):
            kind = 2 * line + (0 if up else 1)
            behind = pos - 1 if up else length - 2 - pos
            last = pos == (length - 1 if up else 0)
            first_one = pos == (0 if up else length - 1)

            def run(k):
                hop(line, up, x.at[k], k).wait_recv()
                if length > 2:
                    @pl.when(jnp.logical_not(last))
                    def _():
                        outs[kind, k] = x[k] + ins[kind, k]
                        hop(line, up, outs.at[kind, k], k).start()

            guarded(t - LAG * behind, jnp.logical_not(first_one), run)

        @pl.when(2 * pos < length)
        def _():
            go(True)
            go(False)

        @pl.when(2 * pos >= length)
        def _():
            go(False)
            go(True)

    def finish(line, x, k, total, at):
        pos, length, _ = lines[line]
        if length == 1:
            total[at] = x[k]
            return
        low, high = ins.at[2 * line], ins.at[2 * line + 1]

        @pl.when(pos == 0)
        def _():
            total[at] = x[k] + high[k]

        @pl.when(pos == length - 1)
        def _():
            total[at] = x[k] + low[k]

        if length > 2:
            @pl.when((pos > 0) & (pos < length - 1))
            def _():
                total[at] = x[k] + low[k] + high[k]

    def send_across(k, carry):
        across(k).start()
        return carry

    lax.fori_loop(0, half, send_across, 0)

    @pl.when(me < size - 1)
    def _():
        to_after().start()

    @pl.when(me > 0)
    def _():
        to_before().start()

    @pl.when(me == 0)
    def _():
        halo_ref[0:HALO] = jnp.zeros((HALO,) + halo_ref.shape[1:], halo_ref.dtype)

    @pl.when(me == size - 1)
    def _():
        halo_ref[HALO:] = jnp.zeros((HALO,) + halo_ref.shape[1:], halo_ref.dtype)

    ready = LAG
    passed = ready + LAG * max(inner - 2, 0)
    reached = passed + LAG
    done = reached + LAG * max(outer - 2, 0)

    def step(t, carry):
        def enter(k):
            across(k).wait_recv()
            first[k] = pick_ref[core * half + k] + part[k]
            begin(0, first, k)

        def turn(k):
            finish(0, first, k, second, k)
            begin(1, second, k)

        def leave(k):
            finish(1, second, k, out_ref, core * half + k)
            back(k).start()

        guarded(t, True, enter)
        relay(0, first, t - ready)
        guarded(t - passed, True, turn)
        relay(1, second, t - reached)
        guarded(t - done, True, leave)
        return carry

    lax.fori_loop(0, half + done, step, 0)

    def close(k, carry):
        across(k).wait_send()
        other = (1 - core) * half + k
        remote(out_ref.at[other], out_ref.at[other], 1, k, partner).wait_recv()
        back(k).wait_send()
        for line, (pos, length, _) in enumerate(lines):
            if length == 1:
                continue

            @pl.when(pos < length - 1)
            def _():
                hop(line, True, first.at[k], k).wait_send()

            @pl.when(pos > 0)
            def _():
                hop(line, False, first.at[k], k).wait_send()

        return carry

    lax.fori_loop(0, half, close, 0)

    @pl.when(me < size - 1)
    def _():
        to_after().wait_send()
        to_before().wait_recv()

    @pl.when(me > 0)
    def _():
        to_before().wait_send()
        to_after().wait_recv()


def lag_kernel(nwin, nrow, sgroup, spec_ref, valid_ref, src_ref, halo_ref, table_ref, out_ref,
               chan_t, src_t, cross_t, lag):
    nchan, depth, fb = spec_ref.shape
    nsrc = src_ref.shape[0]
    nbins = table_ref.shape[0] // 2
    steps = nbins // fb
    at = pl.program_id(0)

    @pl.when(at < steps)
    def _():
        def turn(x):
            return jnp.transpose(x).astype(jnp.float32)

        for c in range(HALO):
            chan_t[c * fb:(c + 1) * fb] = turn(halo_ref[c])
            far = nchan + HALO + c
            chan_t[far * fb:(far + 1) * fb] = turn(halo_ref[HALO + c])

        def channel(c, carry):
            chan_t[pl.ds(pl.multiple_of((c + HALO) * fb, fb), fb)] = (
                turn(spec_ref[c]) * valid_ref[pl.ds(c, 1)])
            return carry

        lax.fori_loop(0, nchan, channel, 0, unroll=4)
        sign = jnp.where(lax.broadcasted_iota(jnp.int32, (1, depth), 1) < nwin, -1.0, 1.0)

        def source(s, carry):
            x = turn(src_ref[s])
            src_t[pl.ds(pl.multiple_of(s * fb, fb), fb)] = x
            src_t[pl.ds(pl.multiple_of((s + nsrc) * fb, fb), fb)] = (
                pltpu.roll(x, nwin, axis=1) * sign)
            return carry

        lax.fori_loop(0, nsrc, source, 0, unroll=2)

        def one(f, carry):
            right = chan_t[pl.ds(f, nrow, stride=fb)].astype(jnp.bfloat16)
            left = src_t[pl.ds(f, 2 * nsrc, stride=fb)].astype(jnp.bfloat16)
            both = lax.dot_general(left, right, (((1,), (1,)), ((), ())),
                                   preferred_element_type=jnp.float32)
            row = pl.multiple_of((at * fb + f) * 2 * nsrc, 2 * nsrc)
            cross_t[pl.ds(row, 2 * nsrc), 0:nrow] = both * (1.0 / nwin)
            return carry

        lax.fori_loop(0, fb, one, 0, unroll=8)

    @pl.when(at >= steps)
    def _():
        group = at - steps
        rows = []
        for q in range(sgroup):
            s = group * sgroup + q
            re = cross_t[pl.ds(s, nbins, stride=2 * nsrc)]
            im = cross_t[pl.ds(s + nsrc, nbins, stride=2 * nsrc)]
            flat = jnp.concatenate([re, im], axis=0).astype(jnp.bfloat16)
            rows.append(jnp.transpose(flat)[0:nrow])
        lag[...] = jnp.dot(jnp.concatenate(rows, axis=0), table_ref[...],
                           preferred_element_type=jnp.float32)
        for q in range(sgroup):
            base = q * nrow
            total = lag[base:base + nchan] + lag[base + 1:base + 1 + nchan]
            for k in range(2, 2 * HALO + 1):
                total = total + lag[base + k:base + k + nchan]
            out_ref[q] = total / (2 * HALO + 1.0)


def local(size, spectra, valid, sources):
    nchan, _, nwin, nbins = spectra.shape
    nsrc = sources.shape[0]
    depth, nlags = 2 * nwin, 2 * nbins
    spec = spectra.reshape(nchan, depth, nbins)
    flags = valid.astype(jnp.float32)
    flags2 = jnp.concatenate([flags, flags], axis=1)
    vmem = pl.BlockSpec(memory_space=pltpu.VMEM)

    picked = pl.pallas_call(
        functools.partial(pick_kernel, nsrc),
        out_shape=jax.ShapeDtypeStruct((nsrc + 2 * HALO, depth, nbins), jnp.bfloat16),
        in_specs=[pl.BlockSpec(memory_space=pltpu.SMEM), vmem, pl.BlockSpec(memory_space=pl.ANY)],
        out_specs=vmem,
        scratch_shapes=[pltpu.VMEM((nsrc + 2 * HALO, depth, nbins), jnp.bfloat16),
                        pltpu.SemaphoreType.DMA((nsrc + 2 * HALO,))],
        compiler_params=pltpu.CompilerParams(vmem_limit_bytes=24 << 20),
        name="pick",
    )(sources, flags2.T, spec)

    chips = size // 2
    inner = 1
    while (2 * inner) ** 2 <= chips and chips % (2 * inner) == 0:
        inner *= 2
    outer = chips // inner
    cut = 2
    nchunk, crow = nsrc * cut, depth // cut
    half = nchunk // 2
    chunk = lambda *lead: pltpu.VMEM(lead + (crow, nbins), jnp.bfloat16)
    src, halo = pl.pallas_call(
        functools.partial(share_kernel, outer, inner, nchunk),
        out_shape=[jax.ShapeDtypeStruct((nchunk, crow, nbins), jnp.bfloat16),
                   jax.ShapeDtypeStruct((2 * HALO, depth, nbins), jnp.bfloat16)],
        in_specs=[vmem, vmem],
        out_specs=[vmem, vmem],
        scratch_shapes=[chunk(half), chunk(half), chunk(half), chunk(4, half), chunk(4, half),
                        pltpu.SemaphoreType.DMA((6, half)), pltpu.SemaphoreType.DMA((6, half)),
                        pltpu.SemaphoreType.DMA((2,)), pltpu.SemaphoreType.DMA((2,))],
        compiler_params=pltpu.CompilerParams(
            collective_id=0, has_side_effects=True, vmem_limit_bytes=40 << 20),
        name="share",
    )(picked[:nsrc].reshape(nchunk, crow, nbins), picked[nsrc:])
    src = src.reshape(nsrc, depth, nbins)

    fb = 128
    steps = nbins // fb
    sgroup = 4 if nsrc % 4 == 0 else 1
    nrow = -(-(nchan + 2 * HALO) // 16) * 16
    by_f = lambda at: (0, 0, jnp.minimum(at, steps - 1))
    return pl.pallas_call(
        functools.partial(lag_kernel, nwin, nrow, sgroup),
        grid=(steps + nsrc // sgroup,),
        out_shape=jax.ShapeDtypeStruct((nsrc, nchan, nlags), jnp.float32),
        in_specs=[pl.BlockSpec((nchan, depth, fb), by_f),
                  pl.BlockSpec((nchan, depth), lambda at: (0, 0)),
                  pl.BlockSpec((nsrc, depth, fb), by_f),
                  pl.BlockSpec((2 * HALO, depth, fb), by_f),
                  pl.BlockSpec((nlags, nlags), lambda at: (0, 0))],
        out_specs=pl.BlockSpec((sgroup, nchan, nlags), lambda at: (jnp.maximum(at - steps, 0), 0, 0)),
        scratch_shapes=[pltpu.VMEM((nrow * fb, depth), jnp.float32),
                        pltpu.VMEM((2 * nsrc * fb, depth), jnp.float32),
                        pltpu.VMEM((nbins * 2 * nsrc, 128), jnp.float32),
                        pltpu.VMEM((sgroup * nrow, nlags), jnp.float32)],
        compiler_params=pltpu.CompilerParams(vmem_limit_bytes=56 << 20),
        name="lags",
    )(spec, flags2, src, halo, jnp.asarray(make_table(nbins, nlags)))


def solution(mesh):
    in_specs = (P(("grp", "chan"), None, None, None), P(("grp", "chan"), None), P("grp"))
    out_specs = P("grp", "chan", None)
    return jax.shard_map(functools.partial(local, mesh.shape["chan"]), mesh=mesh,
                         in_specs=in_specs, out_specs=out_specs, check_vma=False)
```

```python
import functools

import jax
import jax.numpy as jnp
import numpy as np
from jax import lax
from jax.experimental import pallas as pl
from jax.experimental.pallas import tpu as pltpu
from jax.sharding import PartitionSpec as P

MESH = pl.DeviceIdType.MESH
HALO = 2
LAG = 2


def make_table(nbins, nlags):
    freq = np.arange(nbins, dtype=np.int64)
    phase = (freq[:, None] * np.arange(nlags, dtype=np.int64)[None, :]) % nlags
    angle = 2.0 * np.pi * phase / nlags
    weight = np.where(freq == 0, 1.0, 2.0) / nlags
    table = np.concatenate([weight[:, None] * np.cos(angle), -weight[:, None] * np.sin(angle)])
    return table.astype(np.float32).astype(jnp.bfloat16)


def pick_kernel(nsrc, src_ref, mask_ref, spec_ref, out_ref, edge_ref, buf, sems):
    nchan = spec_ref.shape[0]
    me = lax.axis_index("chan")
    spots, copies = [], []
    for row in range(nsrc + 2 * HALO):
        if row < nsrc:
            spot = src_ref[row] - me * nchan
        else:
            spot = row - nsrc if row < nsrc + HALO else nchan - 2 * HALO + row - nsrc
        held = jnp.clip(spot, 0, nchan - 1) if row < nsrc else spot
        copy = pltpu.make_async_copy(spec_ref.at[held], buf.at[row], sems.at[row])
        copy.start()
        spots.append(spot)
        copies.append(copy)
    mask = mask_ref[...]
    lane = lax.broadcasted_iota(jnp.int32, mask.shape, 1)
    for row, (spot, copy) in enumerate(zip(spots, copies)):
        column = jnp.sum(jnp.where(lane == spot, mask, 0.0), axis=1, keepdims=True)
        copy.wait()
        masked = (buf[row].astype(jnp.float32) * column).astype(out_ref.dtype)
        if row < nsrc:
            out_ref[row] = masked
        else:
            edge_ref[row - nsrc] = masked


def share_kernel(outer, inner, nchunk, pick_ref, edge_ref, out_ref, halo_ref, part, first, second,
                 ins, outs, send_sem, recv_sem, edge_send, edge_recv):
    half = nchunk // 2
    size = outer * inner * 2
    me = lax.axis_index("chan")
    core, chip = me % 2, me // 2
    j, i = chip % inner, chip // inner
    lines = ((j, inner, 2), (i, outer, 2 * inner))
    partner = me + 1 - 2 * core

    barrier = pltpu.get_barrier_semaphore()

    def greet(there):
        pl.semaphore_signal(barrier, inc=1, device_id={"chan": there}, device_id_type=MESH)

    greet(partner)
    count = jnp.int32(1)
    for pos, length, stride in lines + ((me, size, 1),):
        @pl.when(pos > 0)
        def _():
            greet(me - stride)

        @pl.when(pos < length - 1)
        def _():
            greet(me + stride)

        count = count + (pos > 0).astype(jnp.int32) + (pos < length - 1).astype(jnp.int32)
    pl.semaphore_wait(barrier, count)

    def remote(src, dst, kind, k, there):
        return pltpu.make_async_remote_copy(
            src_ref=src, dst_ref=dst, send_sem=send_sem.at[kind, k], recv_sem=recv_sem.at[kind, k],
            device_id={"chan": there}, device_id_type=MESH)

    def across(k):
        return remote(pick_ref.at[(1 - core) * half + k], part.at[k], 0, k, partner)

    def back(k):
        spot = core * half + k
        return remote(out_ref.at[spot], out_ref.at[spot], 1, k, partner)

    def hop(line, up, src, k):
        pos, length, stride = lines[line]
        kind = 2 + 2 * line + (0 if up else 1)
        there = me + stride if up else me - stride
        return remote(src, ins.at[kind - 2, k], kind, k, there)

    def to_after():
        return pltpu.make_async_remote_copy(
            src_ref=edge_ref.at[pl.ds(HALO, HALO)], dst_ref=halo_ref.at[pl.ds(0, HALO)],
            send_sem=edge_send.at[0], recv_sem=edge_recv.at[0],
            device_id={"chan": me + 1}, device_id_type=MESH)

    def to_before():
        return pltpu.make_async_remote_copy(
            src_ref=edge_ref.at[pl.ds(0, HALO)], dst_ref=halo_ref.at[pl.ds(HALO, HALO)],
            send_sem=edge_send.at[1], recv_sem=edge_recv.at[1],
            device_id={"chan": me - 1}, device_id_type=MESH)

    def begin(line, x, k):
        pos, length, _ = lines[line]
        if length == 1:
            return

        @pl.when(pos == 0)
        def _():
            hop(line, True, x.at[k], k).start()

        @pl.when(pos == length - 1)
        def _():
            hop(line, False, x.at[k], k).start()

    def guarded(k, also, run):
        @pl.when((k >= 0) & (k < half) & also)
        def _():
            run(k)

    def relay(line, x, t):
        pos, length, _ = lines[line]
        if length == 1:
            return

        def go(up):
            kind = 2 * line + (0 if up else 1)
            behind = pos - 1 if up else length - 2 - pos
            last = pos == (length - 1 if up else 0)
            first_one = pos == (0 if up else length - 1)

            def run(k):
                hop(line, up, x.at[k], k).wait_recv()
                if length > 2:
                    @pl.when(jnp.logical_not(last))
                    def _():
                        outs[kind, k] = x[k] + ins[kind, k]
                        hop(line, up, outs.at[kind, k], k).start()

            guarded(t - LAG * behind, jnp.logical_not(first_one), run)

        @pl.when(2 * pos < length)
        def _():
            go(True)
            go(False)

        @pl.when(2 * pos >= length)
        def _():
            go(False)
            go(True)

    def finish(line, x, k, total, at):
        pos, length, _ = lines[line]
        if length == 1:
            total[at] = x[k]
            return
        low, high = ins.at[2 * line], ins.at[2 * line + 1]

        @pl.when(pos == 0)
        def _():
            total[at] = x[k] + high[k]

        @pl.when(pos == length - 1)
        def _():
            total[at] = x[k] + low[k]

        if length > 2:
            @pl.when((pos > 0) & (pos < length - 1))
            def _():
                total[at] = x[k] + low[k] + high[k]

    def send_across(k, carry):
        across(k).start()
        return carry

    lax.fori_loop(0, half, send_across, 0)

    @pl.when(me < size - 1)
    def _():
        to_after().start()

    @pl.when(me > 0)
    def _():
        to_before().start()

    @pl.when(me == 0)
    def _():
        halo_ref[0:HALO] = jnp.zeros((HALO,) + halo_ref.shape[1:], halo_ref.dtype)

    @pl.when(me == size - 1)
    def _():
        halo_ref[HALO:] = jnp.zeros((HALO,) + halo_ref.shape[1:], halo_ref.dtype)

    ready = LAG
    passed = ready + LAG * max(inner - 2, 0)
    reached = passed + LAG
    done = reached + LAG * max(outer - 2, 0)

    def step(t, carry):
        def enter(k):
            across(k).wait_recv()
            first[k] = pick_ref[core * half + k] + part[k]
            begin(0, first, k)

        def turn(k):
            finish(0, first, k, second, k)
            begin(1, second, k)

        def leave(k):
            finish(1, second, k, out_ref, core * half + k)
            back(k).start()

        guarded(t, True, enter)
        relay(0, first, t - ready)
        guarded(t - passed, True, turn)
        relay(1, second, t - reached)
        guarded(t - done, True, leave)
        return carry

    lax.fori_loop(0, half + done, step, 0)

    def close(k, carry):
        across(k).wait_send()
        other = (1 - core) * half + k
        remote(out_ref.at[other], out_ref.at[other], 1, k, partner).wait_recv()
        back(k).wait_send()
        for line, (pos, length, _) in enumerate(lines):
            if length == 1:
                continue

            @pl.when(pos < length - 1)
            def _():
                hop(line, True, first.at[k], k).wait_send()

            @pl.when(pos > 0)
            def _():
                hop(line, False, first.at[k], k).wait_send()

        return carry

    lax.fori_loop(0, half, close, 0)

    @pl.when(me < size - 1)
    def _():
        to_after().wait_send()
        to_before().wait_recv()

    @pl.when(me > 0)
    def _():
        to_before().wait_send()
        to_after().wait_recv()


def lag_kernel(nwin, nrow, sgroup, spec_ref, valid_ref, src_ref, halo_ref, table_ref, out_ref,
               chan_t, src_t, cross_t, lag):
    nchan, depth, fb = spec_ref.shape
    nsrc = src_ref.shape[0]
    nbins = table_ref.shape[0] // 2
    steps = nbins // fb
    at = pl.program_id(0)
    pitch, cpitch = fb + 1, 2 * nsrc + 1

    @pl.when(at < steps)
    def _():
        def turn(x):
            return jnp.transpose(x).astype(jnp.float32)

        for c in range(HALO):
            chan_t[c * pitch:c * pitch + fb] = turn(halo_ref[c])
            far = nchan + HALO + c
            chan_t[far * pitch:far * pitch + fb] = turn(halo_ref[HALO + c])

        def channel(c, carry):
            chan_t[pl.ds((c + HALO) * pitch, fb)] = (
                turn(spec_ref[c]) * valid_ref[pl.ds(c, 1)])
            return carry

        lax.fori_loop(0, nchan, channel, 0, unroll=4)
        sign = jnp.where(lax.broadcasted_iota(jnp.int32, (1, depth), 1) < nwin, -1.0, 1.0)

        def source(s, carry):
            x = turn(src_ref[s])
            src_t[pl.ds(s * pitch, fb)] = x
            src_t[pl.ds((s + nsrc) * pitch, fb)] = (
                pltpu.roll(x, nwin, axis=1) * sign)
            return carry

        lax.fori_loop(0, nsrc, source, 0, unroll=2)

        def one(f, carry):
            right = chan_t[pl.ds(f, nrow, stride=pitch)].astype(jnp.bfloat16)
            left = src_t[pl.ds(f, 2 * nsrc, stride=pitch)].astype(jnp.bfloat16)
            both = lax.dot_general(left, right, (((1,), (1,)), ((), ())),
                                   preferred_element_type=jnp.float32)
            row = (at * fb + f) * cpitch
            cross_t[pl.ds(row, 2 * nsrc), 0:nrow] = both * (1.0 / nwin)
            return carry

        lax.fori_loop(0, fb, one, 0, unroll=8)

    @pl.when(at >= steps)
    def _():
        group = at - steps
        rows = []
        for q in range(sgroup):
            s = group * sgroup + q
            re = cross_t[pl.ds(s, nbins, stride=cpitch)]
            im = cross_t[pl.ds(s + nsrc, nbins, stride=cpitch)]
            flat = jnp.concatenate([re, im], axis=0).astype(jnp.bfloat16)
            rows.append(jnp.transpose(flat)[0:nrow])
        lags = jnp.dot(jnp.concatenate(rows, axis=0), table_ref[...],
                       preferred_element_type=jnp.float32)
        for n in range(lag.shape[0]):
            lag[n] = lags[:, n * 128:(n + 1) * 128]
        for q in range(sgroup):
            base = q * nrow
            for n in range(lag.shape[0]):
                total = lag[n, base:base + nchan] + lag[n, base + 1:base + 1 + nchan]
                for k in range(2, 2 * HALO + 1):
                    total = total + lag[n, base + k:base + k + nchan]
                out_ref[q, :, n * 128:(n + 1) * 128] = total / (2 * HALO + 1.0)


def local(size, spectra, valid, sources):
    nchan, _, nwin, nbins = spectra.shape
    nsrc = sources.shape[0]
    depth, nlags = 2 * nwin, 2 * nbins
    spec = spectra.reshape(nchan, depth, nbins)
    flags = valid.astype(jnp.float32)
    flags2 = jnp.concatenate([flags, flags], axis=1)
    vmem = pl.BlockSpec(memory_space=pltpu.VMEM)

    picked, edges = pl.pallas_call(
        functools.partial(pick_kernel, nsrc),
        out_shape=[jax.ShapeDtypeStruct((nsrc, depth, nbins), jnp.bfloat16),
                   jax.ShapeDtypeStruct((2 * HALO, depth, nbins), jnp.bfloat16)],
        in_specs=[pl.BlockSpec(memory_space=pltpu.SMEM), vmem, pl.BlockSpec(memory_space=pltpu.MemorySpace.HBM)],
        out_specs=[vmem, vmem],
        scratch_shapes=[pltpu.VMEM((nsrc + 2 * HALO, depth, nbins), jnp.bfloat16),
                        pltpu.SemaphoreType.DMA((nsrc + 2 * HALO,))],
        compiler_params=pltpu.CompilerParams(vmem_limit_bytes=60 << 20),
        name="pick",
    )(sources, flags2.T, spec)

    chips = size // 2
    inner = 1
    while (2 * inner) ** 2 <= chips and chips % (2 * inner) == 0:
        inner *= 2
    outer = chips // inner
    cut = 2
    nchunk, crow = nsrc * cut, depth // cut
    half = nchunk // 2
    chunk = lambda *lead: pltpu.VMEM(lead + (crow, nbins), jnp.bfloat16)
    src, halo = pl.pallas_call(
        functools.partial(share_kernel, outer, inner, nchunk),
        out_shape=[jax.ShapeDtypeStruct((nchunk, crow, nbins), jnp.bfloat16),
                   jax.ShapeDtypeStruct((2 * HALO, depth, nbins), jnp.bfloat16)],
        in_specs=[vmem, vmem],
        out_specs=[vmem, vmem],
        scratch_shapes=[chunk(half), chunk(half), chunk(half), chunk(4, half), chunk(4, half),
                        pltpu.SemaphoreType.DMA((6, half)), pltpu.SemaphoreType.DMA((6, half)),
                        pltpu.SemaphoreType.DMA((2,)), pltpu.SemaphoreType.DMA((2,))],
        compiler_params=pltpu.CompilerParams(
            collective_id=0, has_side_effects=True, vmem_limit_bytes=24 << 20),
        name="share",
    )(picked.reshape(nchunk, crow, nbins), edges)
    src = src.reshape(nsrc, depth, nbins)

    fb = 128
    steps = nbins // fb
    sgroup = 4 if nsrc % 4 == 0 else 1
    nrow = -(-(nchan + 2 * HALO) // 16) * 16
    by_f = lambda at: (0, 0, jnp.minimum(at, steps - 1))
    return pl.pallas_call(
        functools.partial(lag_kernel, nwin, nrow, sgroup),
        grid=(steps + nsrc // sgroup,),
        out_shape=jax.ShapeDtypeStruct((nsrc, nchan, nlags), jnp.float32),
        in_specs=[pl.BlockSpec((nchan, depth, fb), by_f),
                  pl.BlockSpec((nchan, depth), lambda at: (0, 0)),
                  pl.BlockSpec((nsrc, depth, fb), by_f),
                  pl.BlockSpec((2 * HALO, depth, fb), by_f),
                  pl.BlockSpec((nlags, nlags), lambda at: (0, 0))],
        out_specs=pl.BlockSpec((sgroup, nchan, nlags), lambda at: (jnp.maximum(at - steps, 0), 0, 0)),
        scratch_shapes=[pltpu.VMEM((nrow * (fb + 1), depth), jnp.float32),
                        pltpu.VMEM((2 * nsrc * (fb + 1), depth), jnp.float32),
                        pltpu.VMEM((nbins * (2 * nsrc + 1), 128), jnp.float32),
                        pltpu.VMEM((nlags // 128, sgroup * nrow, 128), jnp.float32)],
        compiler_params=pltpu.CompilerParams(vmem_limit_bytes=38 << 20),
        name="lags",
    )(spec, flags2, src, halo, jnp.asarray(make_table(nbins, nlags)))


def solution(mesh):
    in_specs = (P(("grp", "chan"), None, None, None), P(("grp", "chan"), None), P("grp"))
    out_specs = P("grp", "chan", None)
    return jax.shard_map(functools.partial(local, mesh.shape["chan"]), mesh=mesh,
                         in_specs=in_specs, out_specs=out_specs, check_vma=False)
```

```python
import functools

import jax
import jax.numpy as jnp
import numpy as np
from jax import lax
from jax.experimental import pallas as pl
from jax.experimental.pallas import tpu as pltpu
from jax.sharding import PartitionSpec as P

MESH = pl.DeviceIdType.MESH
HALO = 2
LAG = 4


def make_table(nbins, nlags):
    freq = np.arange(nbins, dtype=np.int64)
    phase = (freq[:, None] * np.arange(nlags, dtype=np.int64)[None, :]) % nlags
    angle = 2.0 * np.pi * phase / nlags
    weight = np.where(freq == 0, 1.0, 2.0) / nlags
    table = np.concatenate([weight[:, None] * np.cos(angle), -weight[:, None] * np.sin(angle)])
    return table.astype(np.float32).astype(jnp.bfloat16)


def pick_kernel(nsrc, src_ref, mask_ref, spec_ref, out_ref, edge_ref, buf, sems):
    nchan = spec_ref.shape[0]
    me = lax.axis_index("chan")
    spots, copies = [], []
    for row in range(nsrc + 2 * HALO):
        if row < nsrc:
            spot = src_ref[row] - me * nchan
        else:
            spot = row - nsrc if row < nsrc + HALO else nchan - 2 * HALO + row - nsrc
        held = jnp.clip(spot, 0, nchan - 1) if row < nsrc else spot
        copy = pltpu.make_async_copy(spec_ref.at[held], buf.at[row], sems.at[row])
        copy.start()
        spots.append(spot)
        copies.append(copy)
    mask = mask_ref[...]
    lane = lax.broadcasted_iota(jnp.int32, mask.shape, 1)
    for row, (spot, copy) in enumerate(zip(spots, copies)):
        column = jnp.sum(jnp.where(lane == spot, mask, 0.0), axis=1, keepdims=True)
        copy.wait()
        masked = (buf[row].astype(jnp.float32) * column).astype(out_ref.dtype)
        if row < nsrc:
            out_ref[row] = masked
        else:
            edge_ref[row - nsrc] = masked


def share_kernel(outer, inner, nchunk, pick_ref, edge_ref, out_ref, halo_ref, part, first, second,
                 ins, outs, send_sem, recv_sem, edge_send, edge_recv):
    half = nchunk // 2
    size = outer * inner * 2
    me = lax.axis_index("chan")
    core, chip = me % 2, me // 2
    j, i = chip % inner, chip // inner
    lines = ((j, inner, 2), (i, outer, 2 * inner))
    partner = me + 1 - 2 * core

    barrier = pltpu.get_barrier_semaphore()

    def greet(there):
        pl.semaphore_signal(barrier, inc=1, device_id={"chan": there}, device_id_type=MESH)

    greet(partner)
    count = jnp.int32(1)
    for pos, length, stride in lines + ((me, size, 1),):
        @pl.when(pos > 0)
        def _():
            greet(me - stride)

        @pl.when(pos < length - 1)
        def _():
            greet(me + stride)

        count = count + (pos > 0).astype(jnp.int32) + (pos < length - 1).astype(jnp.int32)
    pl.semaphore_wait(barrier, count)

    def remote(src, dst, kind, k, there):
        return pltpu.make_async_remote_copy(
            src_ref=src, dst_ref=dst, send_sem=send_sem.at[kind, k], recv_sem=recv_sem.at[kind, k],
            device_id={"chan": there}, device_id_type=MESH)

    def across(k):
        return remote(pick_ref.at[(1 - core) * half + k], part.at[k], 0, k, partner)

    def back(k):
        spot = core * half + k
        return remote(out_ref.at[spot], out_ref.at[spot], 1, k, partner)

    def hop(line, up, src, k):
        pos, length, stride = lines[line]
        kind = 2 + 2 * line + (0 if up else 1)
        there = me + stride if up else me - stride
        return remote(src, ins.at[kind - 2, k], kind, k, there)

    def to_after():
        return pltpu.make_async_remote_copy(
            src_ref=edge_ref.at[pl.ds(HALO, HALO)], dst_ref=halo_ref.at[pl.ds(0, HALO)],
            send_sem=edge_send.at[0], recv_sem=edge_recv.at[0],
            device_id={"chan": me + 1}, device_id_type=MESH)

    def to_before():
        return pltpu.make_async_remote_copy(
            src_ref=edge_ref.at[pl.ds(0, HALO)], dst_ref=halo_ref.at[pl.ds(HALO, HALO)],
            send_sem=edge_send.at[1], recv_sem=edge_recv.at[1],
            device_id={"chan": me - 1}, device_id_type=MESH)

    def begin(line, x, k):
        pos, length, _ = lines[line]
        if length == 1:
            return

        @pl.when(pos == 0)
        def _():
            hop(line, True, x.at[k], k).start()

        @pl.when(pos == length - 1)
        def _():
            hop(line, False, x.at[k], k).start()

    def guarded(k, also, run):
        @pl.when((k >= 0) & (k < half) & also)
        def _():
            run(k)

    def relay(line, x, t):
        pos, length, _ = lines[line]
        if length == 1:
            return

        def go(up):
            kind = 2 * line + (0 if up else 1)
            behind = pos - 1 if up else length - 2 - pos
            last = pos == (length - 1 if up else 0)
            first_one = pos == (0 if up else length - 1)

            def run(k):
                hop(line, up, x.at[k], k).wait_recv()
                if length > 2:
                    @pl.when(jnp.logical_not(last))
                    def _():
                        outs[kind, k] = x[k] + ins[kind, k]
                        hop(line, up, outs.at[kind, k], k).start()

            guarded(t - LAG * behind, jnp.logical_not(first_one), run)

        @pl.when(2 * pos < length)
        def _():
            go(True)
            go(False)

        @pl.when(2 * pos >= length)
        def _():
            go(False)
            go(True)

    def finish(line, x, k, total, at):
        pos, length, _ = lines[line]
        if length == 1:
            total[at] = x[k]
            return
        low, high = ins.at[2 * line], ins.at[2 * line + 1]

        @pl.when(pos == 0)
        def _():
            total[at] = x[k] + high[k]

        @pl.when(pos == length - 1)
        def _():
            total[at] = x[k] + low[k]

        if length > 2:
            @pl.when((pos > 0) & (pos < length - 1))
            def _():
                total[at] = x[k] + low[k] + high[k]

    def send_across(k, carry):
        across(k).start()
        return carry

    lax.fori_loop(0, half, send_across, 0)

    @pl.when(me == 0)
    def _():
        halo_ref[0:HALO] = jnp.zeros((HALO,) + halo_ref.shape[1:], halo_ref.dtype)

    @pl.when(me == size - 1)
    def _():
        halo_ref[HALO:] = jnp.zeros((HALO,) + halo_ref.shape[1:], halo_ref.dtype)

    ready = LAG
    passed = ready + LAG * max(inner - 2, 0)
    reached = passed + LAG
    done = reached + LAG * max(outer - 2, 0)

    def step(t, carry):
        def enter(k):
            across(k).wait_recv()
            first[k] = pick_ref[core * half + k] + part[k]
            begin(0, first, k)

        def turn(k):
            finish(0, first, k, second, k)
            begin(1, second, k)

        def leave(k):
            finish(1, second, k, out_ref, core * half + k)
            back(k).start()

        @pl.when(t == half)
        def _():
            @pl.when(me < size - 1)
            def _():
                to_after().start()

            @pl.when(me > 0)
            def _():
                to_before().start()

        guarded(t, True, enter)
        relay(0, first, t - ready)
        guarded(t - passed, True, turn)
        relay(1, second, t - reached)
        guarded(t - done, True, leave)
        return carry

    lax.fori_loop(0, half + done, step, 0)

    def close(k, carry):
        across(k).wait_send()
        other = (1 - core) * half + k
        remote(out_ref.at[other], out_ref.at[other], 1, k, partner).wait_recv()
        back(k).wait_send()
        for line, (pos, length, _) in enumerate(lines):
            if length == 1:
                continue

            @pl.when(pos < length - 1)
            def _():
                hop(line, True, first.at[k], k).wait_send()

            @pl.when(pos > 0)
            def _():
                hop(line, False, first.at[k], k).wait_send()

        return carry

    lax.fori_loop(0, half, close, 0)

    @pl.when(me < size - 1)
    def _():
        to_after().wait_send()
        to_before().wait_recv()

    @pl.when(me > 0)
    def _():
        to_before().wait_send()
        to_after().wait_recv()


def lag_kernel(nwin, nrow, sgroup, spec_ref, valid_ref, src_ref, halo_ref, table_ref, out_ref,
               chan_t, src_t, cross_t, lag):
    nchan, depth, fb = spec_ref.shape
    nsrc = src_ref.shape[0]
    nbins = table_ref.shape[0] // 2
    steps = nbins // fb
    at = pl.program_id(0)
    pitch, cpitch = fb + 1, 2 * nsrc + 1

    @pl.when(at < steps)
    def _():
        def turn(x):
            return jnp.transpose(x).astype(jnp.float32)

        for c in range(HALO):
            chan_t[c * pitch:c * pitch + fb] = turn(halo_ref[c])
            far = nchan + HALO + c
            chan_t[far * pitch:far * pitch + fb] = turn(halo_ref[HALO + c])

        def channel(c, carry):
            chan_t[pl.ds((c + HALO) * pitch, fb)] = (
                turn(spec_ref[c]) * valid_ref[pl.ds(c, 1)])
            return carry

        lax.fori_loop(0, nchan, channel, 0, unroll=4)
        sign = jnp.where(lax.broadcasted_iota(jnp.int32, (1, depth), 1) < nwin, -1.0, 1.0)

        def source(s, carry):
            x = turn(src_ref[s])
            src_t[pl.ds(s * pitch, fb)] = x
            src_t[pl.ds((s + nsrc) * pitch, fb)] = (
                pltpu.roll(x, nwin, axis=1) * sign)
            return carry

        lax.fori_loop(0, nsrc, source, 0, unroll=2)

        def one(f, carry):
            right = chan_t[pl.ds(f, nrow, stride=pitch)].astype(jnp.bfloat16)
            left = src_t[pl.ds(f, 2 * nsrc, stride=pitch)].astype(jnp.bfloat16)
            both = lax.dot_general(left, right, (((1,), (1,)), ((), ())),
                                   preferred_element_type=jnp.float32)
            row = (at * fb + f) * cpitch
            cross_t[pl.ds(row, 2 * nsrc), 0:nrow] = both * (1.0 / nwin)
            return carry

        lax.fori_loop(0, fb, one, 0, unroll=8)

    @pl.when(at >= steps)
    def _():
        group = at - steps
        rows = []
        for q in range(sgroup):
            s = group * sgroup + q
            re = cross_t[pl.ds(s, nbins, stride=cpitch)]
            im = cross_t[pl.ds(s + nsrc, nbins, stride=cpitch)]
            flat = jnp.concatenate([re, im], axis=0).astype(jnp.bfloat16)
            rows.append(jnp.transpose(flat)[0:nrow])
        lags = jnp.dot(jnp.concatenate(rows, axis=0), table_ref[...],
                       preferred_element_type=jnp.float32)
        for n in range(lag.shape[0]):
            lag[n] = lags[:, n * 128:(n + 1) * 128]
        for q in range(sgroup):
            base = q * nrow
            for n in range(lag.shape[0]):
                total = lag[n, base:base + nchan] + lag[n, base + 1:base + 1 + nchan]
                for k in range(2, 2 * HALO + 1):
                    total = total + lag[n, base + k:base + k + nchan]
                out_ref[q, :, n * 128:(n + 1) * 128] = total / (2 * HALO + 1.0)


def local(size, spectra, valid, sources):
    nchan, _, nwin, nbins = spectra.shape
    nsrc = sources.shape[0]
    depth, nlags = 2 * nwin, 2 * nbins
    spec = spectra.reshape(nchan, depth, nbins)
    flags = valid.astype(jnp.float32)
    flags2 = jnp.concatenate([flags, flags], axis=1)
    vmem = pl.BlockSpec(memory_space=pltpu.VMEM)

    picked, edges = pl.pallas_call(
        functools.partial(pick_kernel, nsrc),
        out_shape=[jax.ShapeDtypeStruct((nsrc, depth, nbins), jnp.bfloat16),
                   jax.ShapeDtypeStruct((2 * HALO, depth, nbins), jnp.bfloat16)],
        in_specs=[pl.BlockSpec(memory_space=pltpu.SMEM), vmem, pl.BlockSpec(memory_space=pltpu.MemorySpace.HBM)],
        out_specs=[vmem, vmem],
        scratch_shapes=[pltpu.VMEM((nsrc + 2 * HALO, depth, nbins), jnp.bfloat16),
                        pltpu.SemaphoreType.DMA((nsrc + 2 * HALO,))],
        compiler_params=pltpu.CompilerParams(vmem_limit_bytes=57 << 20),
        name="pick",
    )(sources, flags2.T, spec)

    chips = size // 2
    inner = 1
    while (2 * inner) ** 2 <= chips and chips % (2 * inner) == 0:
        inner *= 2
    outer = chips // inner
    cut = 4
    nchunk, crow = nsrc * cut, depth // cut
    half = nchunk // 2
    chunk = lambda *lead: pltpu.VMEM(lead + (crow, nbins), jnp.bfloat16)
    src, halo = pl.pallas_call(
        functools.partial(share_kernel, outer, inner, nchunk),
        out_shape=[jax.ShapeDtypeStruct((nchunk, crow, nbins), jnp.bfloat16),
                   jax.ShapeDtypeStruct((2 * HALO, depth, nbins), jnp.bfloat16)],
        in_specs=[vmem, vmem],
        out_specs=[vmem, vmem],
        scratch_shapes=[chunk(half), chunk(half), chunk(half), chunk(4, half), chunk(4, half),
                        pltpu.SemaphoreType.DMA((6, half)), pltpu.SemaphoreType.DMA((6, half)),
                        pltpu.SemaphoreType.DMA((2,)), pltpu.SemaphoreType.DMA((2,))],
        compiler_params=pltpu.CompilerParams(
            collective_id=0, has_side_effects=True, vmem_limit_bytes=24 << 20),
        name="share",
    )(picked.reshape(nchunk, crow, nbins), edges)
    src = src.reshape(nsrc, depth, nbins)

    fb = 128
    steps = nbins // fb
    sgroup = 4 if nsrc % 4 == 0 else 1
    nrow = -(-(nchan + 2 * HALO) // 16) * 16
    by_f = lambda at: (0, 0, jnp.minimum(at, steps - 1))
    return pl.pallas_call(
        functools.partial(lag_kernel, nwin, nrow, sgroup),
        grid=(steps + nsrc // sgroup,),
        out_shape=jax.ShapeDtypeStruct((nsrc, nchan, nlags), jnp.float32),
        in_specs=[pl.BlockSpec((nchan, depth, fb), by_f),
                  pl.BlockSpec((nchan, depth), lambda at: (0, 0)),
                  pl.BlockSpec((nsrc, depth, fb), by_f),
                  pl.BlockSpec((2 * HALO, depth, fb), by_f),
                  pl.BlockSpec((nlags, nlags), lambda at: (0, 0))],
        out_specs=pl.BlockSpec((sgroup, nchan, nlags), lambda at: (jnp.maximum(at - steps, 0), 0, 0)),
        scratch_shapes=[pltpu.VMEM((nrow * (fb + 1), depth), jnp.float32),
                        pltpu.VMEM((2 * nsrc * (fb + 1), depth), jnp.float32),
                        pltpu.VMEM((nbins * (2 * nsrc + 1), 128), jnp.float32),
                        pltpu.VMEM((nlags // 128, sgroup * nrow, 128), jnp.float32)],
        compiler_params=pltpu.CompilerParams(vmem_limit_bytes=56 << 20),
        name="lags",
    )(spec, flags2, src, halo, jnp.asarray(make_table(nbins, nlags)))


def solution(mesh):
    in_specs = (P(("grp", "chan"), None, None, None), P(("grp", "chan"), None), P("grp"))
    out_specs = P("grp", "chan", None)
    return jax.shard_map(functools.partial(local, mesh.shape["chan"]), mesh=mesh,
                         in_specs=in_specs, out_specs=out_specs, check_vma=False)
```
